32 devices in a mesh: dp: 16 (over z, y, x), mp: 2 (over core).
Axes of the slice: x: 2, y: 2, z: 4, core: 2. Of those that a mesh axis runs over, the one named last changes fastest.
Arguments:
- tokens: bfloat16 [4096, 768], P(('dp', 'mp')), may hold values from -6 to 6
- attn_gain: bfloat16 [768], P(('dp', 'mp')), may hold values from 0.5 to 1.5
- w_query: bfloat16 [768, 768], P('dp', 'mp'), may hold values from -0.21875 to 0.21875
- w_key: bfloat16 [768, 768], P('dp', 'mp'), may hold values from -0.21875 to 0.21875
- w_value: bfloat16 [768, 768], P('dp', 'mp'), may hold values from -0.21875 to 0.21875
- w_proj: bfloat16 [768, 768], P('mp', 'dp'), may hold values from -0.625 to 0.625
- rel_table: float32 [32, 12], P(None, 'mp'), may hold values from -4 to 4
- rel_bucket: int32 [256], replicated, may hold values from 0 to 31, as said below
- segments: int32 [4096], P('dp'), may hold values from 0 to 63, never falling along the last dimension, each value on 1 to 256 neighbouring positions
- ffn_gain: bfloat16 [768], P(('dp', 'mp')), may hold values from 0.5 to 1.5
- router: bfloat16 [768, 8], P(('dp', 'mp')), may hold values from -0.15625 to 0.15625
- expert_ids: int32 [4096, 2], P('dp'), may hold values from 0 to 7, all different within a row
- expert_in: bfloat16 [16, 768, 1536], P('dp', None, 'mp'), may hold values from -0.21875 to 0.21875
- expert_out: bfloat16 [16, 1536, 768], P('dp', 'mp'), may hold values from -0.109375 to 0.109375
- cotangent: bfloat16 [4096, 768], P(('dp', 'mp')), may hold values from -6 to 6
Outputs:
- layer_out: bfloat16 [4096, 768], P(('dp', 'mp'))
- grad_tokens: float32 [4096, 768], P(('dp', 'mp'))
- grad_attn_gain: float32 [768], P(('dp', 'mp'))
- grad_query: float32 [768, 768], P('dp', 'mp')
- grad_key: float32 [768, 768], P('dp', 'mp')
- grad_value: float32 [768, 768], P('dp', 'mp')
- grad_proj: float32 [768, 768], P('mp', 'dp')
- grad_table: float32 [32, 12], P(None, 'mp')
- grad_ffn_gain: float32 [768], P(('dp', 'mp'))
- grad_router: float32 [768, 8], P(('dp', 'mp'))
- grad_expert_in: float32 [16, 768, 1536], P('dp', None, 'mp')
- grad_expert_out: float32 [16, 1536, 768], P('dp', 'mp')
The draws below stay inside these ranges and needn't reach their ends.
Inputs may be any that keep to these rules, and one draw needn't show every extreme that they name: `expert_ids`: each token names two different experts. `segments`: document numbers never fall along the tokens; a document may run on into the next sequence. `rel_bucket`: never falls as the distance grows; 0 at distance 0 and 31 at distance 256 - 1.
All inputs are finite; a program needn't handle non-finite values.
Results may differ from the reference program's by a relative error of at most 0.02.
Values may be sent and summed in bfloat16 or wider, within the bound.
A program may use at most 128 MiB of HBM per device.

```python
import math
import jax
import jax.numpy as jnp
import numpy as np
from jax import lax

D = 768
HEADS = 12
HEAD_DIM = 64
FF = 3072
NB = 32
SEQ = 256
SEQS = 16
TOKENS = 4096
EXPERTS = 8
CAP = 72


def draw_rel_bucket(key, part):
    coin_flips = jax.random.randint(key, (SEQ,), 0, 4)
    distance = jnp.arange(SEQ, dtype=jnp.int32)
    step_ups = jnp.where(distance < NB // 2, 1, (coin_flips == 0).astype(jnp.int32))
    step_ups = jnp.where(distance == 0, 0, step_ups).astype(jnp.int32)
    bucket = jnp.minimum(jnp.cumsum(step_ups, dtype=jnp.int32), NB - 1)
    return bucket.at[SEQ - 1].set(NB - 1).astype(jnp.int32)


def block_scale(stream_key, dims, cuts, low, high):
    loudness, own = 1.0, jax.random.fold_in(stream_key, 6)
    for position, blocks in cuts:
        draws = jnp.exp(jax.random.uniform(jax.random.fold_in(own, position), (blocks,), jnp.float32, low / len(cuts), high / len(cuts)))
        loudness = loudness * jnp.repeat(draws, dims[position] // blocks).reshape([-1 if axis == position else 1 for axis in range(len(dims))])
    return loudness


def distinct(stream_key, rows, amount, top, lift):
    order = jax.random.permutation(jax.random.fold_in(stream_key, 1), amount)
    boost = order
    for power in range(3):
        boost = boost * boost // amount
    boost = boost * lift // amount
    tickets = jax.random.randint(jax.random.fold_in(stream_key, 2), (rows, amount), 0, 4096) + boost
    holders = jax.random.permutation(jax.random.fold_in(stream_key, 3), rows)[jnp.arange(amount) % rows]
    tickets = jnp.where(jnp.arange(rows)[:, None] == holders[None, :], 1 << 14, tickets)
    merit = tickets * amount + jnp.arange(amount)
    return lax.top_k(merit.astype(jnp.int32), top)[1].astype(jnp.int32)


def profile(number_of, total, reach, lean):
    weights = [(1 << 20) // math.isqrt(standing ** lean) + 1 for standing in range(2, number_of + 1)]
    rest, counts = total - reach - (number_of - 1), [1] * (number_of - 1)
    while rest > 0:
        movable = [i for i in range(number_of - 1) if counts[i] < reach]
        mass, remaining = sum([weights[i] for i in movable]), rest
        for i in movable:
            addition = min(reach - counts[i], max(1, remaining * weights[i] // mass), rest)
            counts[i] = counts[i] + addition
            rest = rest - addition
    return np.array([reach] + counts)


def ragged(own_key, count, total, bound, lean):
    if count == 2:
        one = jax.random.randint(own_key, (), max(1, total - bound), min(bound, total - 1) + 1)
        return jnp.stack([one, total - one])
    lengths = jnp.asarray(profile(count, total, bound, lean), jnp.int32)
    couples = (count - 1) // 2
    source_of, receiver = lengths[1:1 + 2 * couples:2], lengths[2:2 + 2 * couples:2]
    room = jnp.minimum(source_of - 1, bound - receiver)
    shifted = jax.random.randint(jax.random.fold_in(own_key, 1), (couples,), 0, 1 << 20) % (room + 1)
    lengths = lengths.at[1:1 + 2 * couples:2].set(source_of - shifted).at[2:2 + 2 * couples:2].set(receiver + shifted)
    return lengths[jax.random.permutation(jax.random.fold_in(own_key, 2), count)]


def noise(own_key, shape, spread, bound, split=(), kind=jnp.bfloat16):
    drawn = jax.random.normal(own_key, shape, jnp.float32) * spread
    if len(split) > 0:
        drawn = block_scale(own_key, shape, split, -0.22, 0.18) * drawn
    return jnp.clip(drawn, min=-bound, max=bound).astype(kind)


def setup_inputs(seed: int = 0) -> dict:
    keys = jax.random.split(jax.random.key(seed), 16)
    return {
        "tokens": noise(keys[0], (TOKENS, D), 1.0, 6.0, ((0, 32),)),
        "attn_gain": jnp.clip(1.0 + 0.1 * jax.random.normal(keys[1], (D,), jnp.float32), 0.5, 1.5).astype(jnp.bfloat16),
        "w_query": noise(keys[2], (D, D), D ** -0.5, 0.21875, ((0, 16), (1, 2))),
        "w_key": noise(keys[3], (D, D), D ** -0.5, 0.21875, ((0, 16), (1, 2))),
        "w_value": noise(keys[4], (D, D), D ** -0.5, 0.21875, ((0, 16), (1, 2))),
        "w_proj": noise(keys[5], (D, D), (D // 8) ** -0.5, 0.625, ((0, 2), (1, 16))),
        "rel_table": noise(keys[6], (NB, HEADS), 1.0, 4.0, ((1, 2),), jnp.float32),
        "rel_bucket": draw_rel_bucket(jax.random.fold_in(keys[15], 71), 0),
        "segments": jnp.searchsorted(jnp.cumsum(ragged(keys[8], 4 * SEQS, TOKENS, SEQ, 2)), jnp.arange(TOKENS), side="right").astype(jnp.int32),
        "ffn_gain": jnp.clip(1.0 + 0.1 * jax.random.normal(keys[9], (D,), jnp.float32), 0.5, 1.5).astype(jnp.bfloat16),
        "router": noise(keys[10], (D, EXPERTS), (2 * D) ** -0.5, 0.15625, ((0, 32),)),
        "expert_ids": distinct(keys[11], TOKENS, EXPERTS, 2, 2048),
        "expert_in": noise(keys[12], (2 * EXPERTS, D, FF // 2), D ** -0.5, 0.21875, ((0, 16), (2, 2))),
        "expert_out": noise(keys[13], (2 * EXPERTS, FF // 2, D), FF ** -0.5, 0.109375, ((0, 16), (1, 2))),
        "cotangent": noise(keys[14], (TOKENS, D), 1.0, 6.0, ((0, 32),)),
    }


EPS = 1e-06
NEGATIVE = -1e+30
HIGH = lax.Precision.HIGHEST

@jax.custom_vjp
def low(v):
    return lax.optimization_barrier(v.astype(jnp.bfloat16)).astype(jnp.float32)

@jax.custom_vjp
def low_back(v):
    return v

def low_keep(v):
    return (low(v), None)

def low_pass(kept, grad):
    return (grad,)

def back_keep(v):
    return (v, None)

def back_low(kept, grad):
    return (low(grad),)
low.defvjp(low_keep, low_pass)
low_back.defvjp(back_keep, back_low)

def matmul(left, right):
    return jnp.dot(left, right, precision=HIGH)

def norm_rows(values, norm_gain):
    return values * lax.rsqrt(lax.optimization_barrier(jnp.mean(values * values, axis=-1, keepdims=True)) + EPS) * norm_gain

def gate_values(logits, routes):
    router_probs = jax.nn.softmax(logits, axis=-1)
    chosen = jnp.take_along_axis(router_probs, routes, axis=1)
    return chosen / lax.optimization_barrier(jnp.sum(chosen, axis=1, keepdims=True))

def slot_plan(routes, experts, capacity):
    flat_ids = routes.reshape(-1).astype(jnp.int32)
    onehot = (flat_ids[:, None] == jnp.arange(experts, dtype=jnp.int32)[None, :]).astype(jnp.int32)
    before = jnp.cumsum(onehot, axis=0, dtype=jnp.int32) - onehot
    slot_place = lax.optimization_barrier(jnp.sum(before * onehot, axis=1, dtype=jnp.int32))
    is_kept = slot_place < capacity
    target = jnp.where(is_kept, flat_ids * capacity + slot_place, experts * capacity).astype(jnp.int32)
    pair_ids = jnp.arange(flat_ids.shape[0], dtype=jnp.int32)
    slot_owner = jnp.zeros((experts * capacity,), jnp.int32).at[target].set(pair_ids, mode='drop')
    filled = jnp.zeros((experts * capacity,), jnp.int32).at[target].set(1, mode='drop')
    return (is_kept, target, slot_owner, filled)

def sequence_forward(params, row_tokens, seg_ids, routes, bucket):
    gain_one, w_query, w_key, w_value, w_proj, bias_table, gain_two, router, expert_in, expert_out = params
    seq_len = row_tokens.shape[0]
    normed_one = low(norm_rows(row_tokens, gain_one))
    queries = low(low_back(matmul(normed_one, w_query))).reshape(seq_len, HEADS, HEAD_DIM)
    key_rows = low(low_back(matmul(normed_one, w_key))).reshape(seq_len, HEADS, HEAD_DIM)
    value_rows = low(low_back(matmul(normed_one, w_value))).reshape(seq_len, HEADS, HEAD_DIM)
    scores = jnp.einsum('qhd,khd->hqk', queries, key_rows, precision=HIGH)
    positions = jnp.arange(seq_len, dtype=jnp.int32)
    distance = positions[:, None] - positions[None, :]
    bias = bias_table[bucket[jnp.clip(distance, 0, seq_len - 1)]]
    logits = low_back(scores * HEAD_DIM ** (-0.5) + jnp.transpose(bias, (2, 0, 1)))
    allowed = (distance >= 0) & (seg_ids[:, None] == seg_ids[None, :])
    logits = jnp.where(allowed[None], logits, NEGATIVE)
    attn_probs = jax.nn.softmax(logits, axis=-1)
    mixed_rows = jnp.einsum('hqk,khd->qhd', low(attn_probs), value_rows, precision=HIGH).reshape(seq_len, D)
    mixed_rows = low(low_back(mixed_rows))
    after_attn = row_tokens + low_back(matmul(mixed_rows, w_proj))
    normed_two = low(norm_rows(after_attn, gain_two))
    router_logits = low_back(matmul(normed_two, router))
    gate_weights = gate_values(router_logits, routes)
    is_kept, target, slot_owner, filled = slot_plan(routes, EXPERTS, CAP)
    slot_rows = normed_two[slot_owner // 2] * filled[:, None].astype(jnp.float32)
    slot_rows = slot_rows.reshape(EXPERTS, CAP, D)
    first_full = expert_in.reshape(EXPERTS, 2, D, FF // 2).transpose(0, 2, 1, 3).reshape(EXPERTS, D, FF)
    second_full = expert_out.reshape(EXPERTS, FF, D)
    pre_act = low_back(jnp.einsum('ecd,edf->ecf', slot_rows, first_full, precision=HIGH))
    hidden = low(jax.nn.gelu(pre_act))
    result = low_back(jnp.einsum('ecf,efd->ecd', hidden, second_full, precision=HIGH)).reshape(EXPERTS * CAP, D)
    per_pair = result[jnp.minimum(target, EXPERTS * CAP - 1)] * is_kept[:, None].astype(jnp.float32)
    per_pair = per_pair.reshape(seq_len, 2, D)
    return after_attn + lax.optimization_barrier(jnp.sum(gate_weights[:, :, None] * per_pair, axis=1))

def forward(params, all_tokens, segments, expert_ids, rel_bucket):
    token_blocks = all_tokens.reshape(SEQS, SEQ, D)
    seg_blocks = segments.reshape(SEQS, SEQ)
    route_blocks = expert_ids.reshape(SEQS, SEQ, 2)
    checked_step = jax.checkpoint(sequence_forward)

    def one_sequence(pieces):
        return checked_step(params, pieces[0], pieces[1], pieces[2], rel_bucket)
    outputs = lax.map(one_sequence, (token_blocks, seg_blocks, route_blocks))
    return outputs.reshape(SEQS * SEQ, D)

def reference(tokens, attn_gain, w_query, w_key, w_value, w_proj, rel_table, rel_bucket, segments, ffn_gain, router, expert_ids, expert_in, expert_out, cotangent):
    floats = tuple((item.astype(jnp.float32) for item in (attn_gain, w_query, w_key, w_value, w_proj, rel_table, ffn_gain, router, expert_in, expert_out)))

    def run_layer(token_values, params):
        return forward(params, token_values, segments, expert_ids, rel_bucket)
    result, pull_back = jax.vjp(run_layer, tokens.astype(jnp.float32), floats)
    token_grad, weight_grads = pull_back(cotangent.astype(jnp.float32))
    return (result.astype(jnp.bfloat16), token_grad, weight_grads[0], weight_grads[1], weight_grads[2], weight_grads[3], weight_grads[4], weight_grads[5], weight_grads[6], weight_grads[7], weight_grads[8], weight_grads[9])
```

```python
import functools

import jax
import jax.numpy as jnp
from jax import lax
from jax.experimental import pallas as pl
from jax.experimental.pallas import tpu as pltpu
from jax.sharding import PartitionSpec as P

MESH = pl.DeviceIdType.MESH
BF16 = jnp.bfloat16
F32 = jnp.float32
EPS = 1e-06
NEGATIVE = -1e30
HIGH = lax.Precision.HIGHEST
UNROLL = 8


def each(count, body):
    if count <= UNROLL:
        for k in range(count):
            body(k)
    else:
        lax.fori_loop(0, count, lambda k, c: (body(k), c)[1], 0)


def bit_orders(n):
    bits = [1 << b for b in range(n.bit_length() - 1)]
    if n == 16:
        return [[8, 4, 2, 1], [2, 8, 1, 4], [1, 8, 4, 2], [8, 4, 1, 2], [8, 4, 2, 1]]
    down = bits[::-1]
    return [down[w % len(bits):] + down[: w % len(bits)] for w in range(5)]


def deltas(d, n):
    return {1 << b: (1 << b) * (1 - 2 * ((d // (1 << b)) % 2)) for b in range(n.bit_length() - 1)}


def spread(k, order, level, step):
    mask, offset = 0, 0
    for j in range(level):
        bit = (k // (1 << j)) % 2
        mask = mask + bit * order[j]
        offset = offset + bit * step[order[j]]
    return mask, offset


def remote(src, dst, send, recv, dev):
    return pltpu.make_async_remote_copy(
        src_ref=src, dst_ref=dst, send_sem=send, recv_sem=recv, device_id=dev, device_id_type=MESH
    )


def greet(peers):
    barrier = pltpu.get_barrier_semaphore()
    for dev in peers:
        pl.semaphore_signal(barrier, inc=1, device_id=dev, device_id_type=MESH)
    pl.semaphore_wait(barrier, len(peers))


def any_spec():
    return pl.BlockSpec(memory_space=pl.ANY)


def vmem_spec():
    return pl.BlockSpec(memory_space=pltpu.VMEM)


def gather_body(n, wq, wk, wv, wp, small, tok, cot, full, sfull, stok, scot, send, recv, lsem, ssend, srecv):
    d = lax.axis_index("dp")
    m = lax.axis_index("mp")
    orders = bit_orders(n)
    levels = n.bit_length() - 1
    step = deltas(d, n)
    sib = {"mp": 1 - m}
    own = [wq, wk, wv, wp]
    locals_ = [
        pltpu.make_async_copy(tok, stok.at[m], lsem.at[0]),
        pltpu.make_async_copy(cot, scot.at[m], lsem.at[1]),
        pltpu.make_async_copy(small, sfull.at[d, m], lsem.at[2]),
    ] + [pltpu.make_async_copy(own[w], full.at[w, d], lsem.at[3 + w]) for w in range(4)]
    for c in locals_:
        c.start()
    greet([sib] + [{"dp": d + step[1 << b]} for b in range(levels)])
    sibs = [
        remote(small, sfull.at[d, m], ssend.at[0], srecv.at[0], sib),
        remote(tok, stok.at[m], ssend.at[1], srecv.at[1], sib),
        remote(cot, scot.at[m], ssend.at[2], srecv.at[2], sib),
    ]
    for c in sibs:
        c.start()

    def part(w, shard):
        return full.at[w, shard] if w < 4 else sfull.at[shard]

    def hop(w, src, shard, sem, bit):
        return remote(src, part(w, shard), send.at[w, sem], recv.at[w, sem], {"dp": d + step[bit]})

    for w in range(4):
        for bit in orders[w]:
            hop(w, own[w], d, bit, bit).start()
    locals_[2].wait()
    sibs[0].wait_recv()
    for bit in orders[4]:
        hop(4, part(4, d), d, bit, bit).start()
    for i in range(levels):
        for w in range(5):
            order = orders[w]

            def pass_on(k, w=w, order=order, i=i):
                mask, offset = spread(k, order, i, step)
                rel = mask + order[i]
                shard = d + offset + step[order[i]]
                hop(w, part(w, shard), shard, rel, order[i]).wait_recv()
                for j in range(i + 1, levels):
                    hop(w, part(w, shard), shard, rel + order[j], order[j]).start()

            each(1 << i, pass_on)

    def drain(k):
        for w in range(5):
            hop(w, part(w, d), d, k + 1, 1).wait_send()

    each(n - 1, drain)
    for c in sibs:
        c.wait_send()
    sibs[1].wait_recv()
    sibs[2].wait_recv()
    for c in locals_[:2] + locals_[3:]:
        c.wait()


def gather_all(n, wq, wk, wv, wp, small, tok, cot):
    rows, width = wq.shape
    return pl.pallas_call(
        functools.partial(gather_body, n),
        name="gather_all",
        out_shape=(
            jax.ShapeDtypeStruct((4, n, rows, width), BF16),
            jax.ShapeDtypeStruct((n, 2) + small.shape, BF16),
            jax.ShapeDtypeStruct((2,) + tok.shape, BF16),
            jax.ShapeDtypeStruct((2,) + cot.shape, BF16),
        ),
        in_specs=[any_spec()] * 7,
        out_specs=(vmem_spec(),) * 4,
        scratch_shapes=[
            pltpu.SemaphoreType.DMA((5, n)),
            pltpu.SemaphoreType.DMA((5, n)),
            pltpu.SemaphoreType.DMA((7,)),
            pltpu.SemaphoreType.DMA((3,)),
            pltpu.SemaphoreType.DMA((3,)),
        ],
        compiler_params=pltpu.CompilerParams(collective_id=0, has_side_effects=True),
    )(wq, wk, wv, wp, small, tok, cot)


def swap_body(x, out, send, recv):
    sib = {"mp": 1 - lax.axis_index("mp")}
    greet([sib])
    copy = remote(x, out, send, recv, sib)
    copy.start()
    copy.wait()


def swap(x, collective_id):
    return pl.pallas_call(
        swap_body,
        name="swap",
        out_shape=jax.ShapeDtypeStruct(x.shape, x.dtype),
        in_specs=[vmem_spec()],
        out_specs=vmem_spec(),
        scratch_shapes=[pltpu.SemaphoreType.DMA, pltpu.SemaphoreType.DMA],
        compiler_params=pltpu.CompilerParams(collective_id=collective_id, has_side_effects=True),
    )(x)


def dispatch_body(n, slots, recv, send, got, lsem):
    d = lax.axis_index("dp")
    m = lax.axis_index("mp")
    experts = n // 2
    cap = slots.shape[2]
    x = d % 2
    mine = d // 2
    sib = {"mp": 1 - m}
    across = {"dp": 2 * mine + (1 - x)}
    barrier = pltpu.get_barrier_semaphore()

    def plane(k):
        return {"dp": 2 * ((mine + k) % experts) + x}

    def hello(k):
        pl.semaphore_signal(barrier, inc=1, device_id=plane(k + 1), device_id_type=MESH)

    for dev in (sib, across):
        pl.semaphore_signal(barrier, inc=1, device_id=dev, device_id_type=MESH)
    each(experts - 1, hello)
    pl.semaphore_wait(barrier, experts + 1)

    def place(kind, src):
        return recv.at[kind * 2 + m, pl.ds(pl.multiple_of(src * cap, 8), cap)]

    def hop(kind, src_ref, src, sem, dev):
        return remote(src_ref, place(kind, src), send.at[kind, sem], got.at[kind, sem], dev)

    def to_plane(k):
        e = (mine + k + 1) % experts
        for kind in range(2):
            hop(kind, slots.at[kind, e], d, k + 1, plane(k + 1)).start()

    each(experts - 1, to_plane)
    for kind in range(2):
        pltpu.make_async_copy(slots.at[kind, mine], place(kind, d), lsem.at[kind]).start()
        hop(kind, slots.at[kind, mine], d, experts, across).start()
        hop(kind, slots.at[kind, mine], d, 2 * experts, sib).start()

    def near(k):
        src = 2 * ((mine + 2 * experts - k - 1) % experts) + x
        for kind in range(2):
            hop(kind, place(kind, src), src, k + 1, sib).wait_recv()
            hop(kind, place(kind, src), src, experts + k + 1, across).start()
            hop(kind, place(kind, src), src, 2 * experts + k + 1, sib).start()

    each(experts - 1, near)

    def far(k):
        src = 2 * ((mine + 2 * experts - k) % experts) + (1 - x)
        for kind in range(2):
            hop(kind, place(kind, src), src, experts + k, across).wait_recv()
            hop(kind, place(kind, src), src, 3 * experts + k, sib).start()

    each(experts, far)

    def drain(k):
        for kind in range(2):
            hop(kind, place(kind, d), d, k + 1, sib).wait_send()

    each(4 * experts - 1, drain)

    def from_sib(k):
        for kind in range(2):
            hop(kind, place(kind, d), d, 2 * experts + k, sib).wait_recv()

    each(2 * experts, from_sib)
    for kind in range(2):
        pltpu.make_async_copy(slots.at[kind, mine], place(kind, d), lsem.at[kind]).wait()


def dispatch(n, slots):
    _, experts, cap, half = slots.shape
    return pl.pallas_call(
        functools.partial(dispatch_body, n),
        name="dispatch",
        out_shape=jax.ShapeDtypeStruct((4, n * cap, half), BF16),
        in_specs=[vmem_spec()],
        out_specs=vmem_spec(),
        scratch_shapes=[
            pltpu.SemaphoreType.DMA((2, 4 * experts)),
            pltpu.SemaphoreType.DMA((2, 4 * experts)),
            pltpu.SemaphoreType.DMA((2,)),
        ],
        compiler_params=pltpu.CompilerParams(collective_id=1, has_side_effects=True),
    )(slots)


def collect_body(n, parts, ret, sib_buf, x_out, x_in, home, send, got, lsem):
    d = lax.axis_index("dp")
    m = lax.axis_index("mp")
    experts = n // 2
    cap = parts.shape[2]
    x = d % 2
    mine = d // 2
    sib = {"mp": 1 - m}
    across = {"dp": 2 * mine + (1 - x)}
    barrier = pltpu.get_barrier_semaphore()

    def plane(k):
        return {"dp": 2 * ((mine + k) % experts) + x}

    def hello(k):
        pl.semaphore_signal(barrier, inc=1, device_id=plane(k + 1), device_id_type=MESH)

    for dev in (sib, across):
        pl.semaphore_signal(barrier, inc=1, device_id=dev, device_id_type=MESH)
    each(experts - 1, hello)
    pl.semaphore_wait(barrier, experts + 1)

    def seq(k, side):
        return 2 * ((mine + k) % experts) + (x if side == 0 else 1 - x)

    def to_sib(kind, k, side):
        sem = side * experts + k
        return remote(
            parts.at[kind * 2 + (1 - m), seq(k, side)], sib_buf.at[kind, side, k],
            send.at[kind, sem], got.at[kind, sem], sib,
        )

    def to_x(kind, k):
        sem = 2 * experts + k
        return remote(x_out.at[kind, k], x_in.at[kind, k], send.at[kind, sem], got.at[kind, sem], across)

    def slot(kind, half, e):
        return ret.at[kind * 2 + half, pl.ds(pl.multiple_of(e * cap, 8), cap)]

    def go_home(kind, k):
        sem = 3 * experts + k
        return remote(
            home.at[kind, k], slot(kind, m, mine), send.at[kind, sem], got.at[kind, sem], plane(k)
        )

    def share(kind, k):
        e = (mine + experts - k) % experts
        sem = 4 * experts + k
        return remote(slot(kind, m, e), slot(kind, m, e), send.at[kind, sem], got.at[kind, sem], sib)

    for side in (1, 0):

        def first(k, side=side):
            for kind in range(2):
                to_sib(kind, k, side).start()

        each(experts, first)

    def second(k):
        for kind in range(2):
            to_sib(kind, k, 1).wait_recv()
            mine_part = parts[kind * 2 + m, seq(k, 1)].astype(F32)
            x_out[kind, k] = (mine_part + sib_buf[kind, 1, k].astype(F32)).astype(BF16)
            to_x(kind, k).start()

    each(experts, second)

    def third(k):
        for kind in range(2):
            to_sib(kind, k, 0).wait_recv()
            to_x(kind, k).wait_recv()
            mine_part = parts[kind * 2 + m, seq(k, 0)].astype(F32)
            both = mine_part + sib_buf[kind, 0, k].astype(F32)
            home[kind, k] = (both + x_in[kind, k].astype(F32)).astype(BF16)

    def third_far(k):
        third(k + 1)
        for kind in range(2):
            go_home(kind, k + 1).start()

    each(experts - 1, third_far)
    third(0)
    for kind in range(2):
        pltpu.make_async_copy(home.at[kind, 0], slot(kind, m, mine), lsem.at[kind]).start()

    def fourth(k):
        for kind in range(2):
            go_home(kind, k + 1).wait_recv()
            share(kind, k + 1).start()

    each(experts - 1, fourth)
    for kind in range(2):
        pltpu.make_async_copy(home.at[kind, 0], slot(kind, m, mine), lsem.at[kind]).wait()
        share(kind, 0).start()

    def drain(k):
        for kind in range(2):
            to_sib(kind, k, 0).wait_send()
            to_sib(kind, k, 1).wait_send()
            to_x(kind, k).wait_send()
            share(kind, k).wait_send()
            share(kind, k).wait_recv()

    each(experts, drain)

    def drain_home(k):
        for kind in range(2):
            go_home(kind, k + 1).wait_send()

    each(experts - 1, drain_home)


def collect(n, parts):
    _, _, cap, half = parts.shape
    experts = n // 2
    return pl.pallas_call(
        functools.partial(collect_body, n),
        name="collect",
        out_shape=jax.ShapeDtypeStruct((4, experts * cap, half), BF16),
        in_specs=[vmem_spec()],
        out_specs=vmem_spec(),
        scratch_shapes=[
            pltpu.VMEM((2, 2, experts, cap, half), BF16),
            pltpu.VMEM((2, experts, cap, half), BF16),
            pltpu.VMEM((2, experts, cap, half), BF16),
            pltpu.VMEM((2, experts, cap, half), BF16),
            pltpu.SemaphoreType.DMA((2, 5 * experts)),
            pltpu.SemaphoreType.DMA((2, 5 * experts)),
            pltpu.SemaphoreType.DMA((2,)),
        ],
        compiler_params=pltpu.CompilerParams(collective_id=2, has_side_effects=True),
    )(parts)


def reduce_body(
    n, gain_col, grads, small, table, rows, gout, sout, tout, rout,
    rbuf, rsmall, sbuf, ssmall, sib_small, tsend, trecv,
    send, got, xsend, xgot,
):
    d = lax.axis_index("dp")
    m = lax.axis_index("mp")
    orders = bit_orders(n)
    levels = n.bit_length() - 1
    step = deltas(d, n)
    sib = {"mp": 1 - m}
    greet([sib] + [{"dp": d + step[1 << b]} for b in range(levels)])
    to_sib = [
        remote(small, sib_small, xsend.at[0], xgot.at[0], sib),
        remote(rows.at[1 - m], rout, xsend.at[1], xgot.at[1], sib),
    ]
    for c in to_sib:
        c.start()

    def landing(w, rel):
        return rbuf.at[w, rel] if w < 4 else rsmall.at[rel]

    def hop(w, src, rel, bit):
        return remote(src, landing(w, rel), send.at[w, rel], got.at[w, rel], {"dp": d + step[bit]})

    def total(w, shard, rel, level):
        if w < 4:
            value = grads[w, shard].astype(F32)
        else:
            value = small[shard].astype(F32)
            column = lax.broadcasted_iota(jnp.int32, value.shape, value.ndim - 1)
            value = value + jnp.where(column == gain_col, sib_small[shard].astype(F32), 0.0)
        for i in range(level, levels):
            at = rel + orders[w][i]
            hop(w, landing(w, at), at, orders[w][i]).wait_recv()
            value = value + (rbuf[w, at] if w < 4 else rsmall[at]).astype(F32)
        return value

    tsend[0] = table[...]
    taround = [
        remote(tsend.at[i], trecv.at[i], xsend.at[2 + i], xgot.at[2 + i], {"dp": d + step[1 << i]})
        for i in range(levels)
    ]
    taround[0].start()
    for i in reversed(range(levels)):
        for w in range(5):
            order = orders[w]
            if w == 4 and i == levels - 1:
                to_sib[0].wait_recv()

            def pass_on(k, w=w, order=order, i=i):
                mask, offset = spread(k, order, i, step)
                rel = mask + order[i]
                shard = d + offset + step[order[i]]
                if i == levels - 1 and w < 4:
                    hop(w, grads.at[w, shard], rel, order[i]).start()
                else:
                    value = total(w, shard, rel, i + 1).astype(BF16)
                    out = sbuf.at[w, rel] if w < 4 else ssmall.at[rel]
                    out[...] = value
                    hop(w, out, rel, order[i]).start()

            each(1 << i, pass_on)
        done = levels - 1 - i
        taround[done].wait_recv()
        value = tsend[done] + trecv[done]
        if done + 1 < levels:
            tsend[done + 1] = value
            taround[done + 1].start()
        else:
            tout[...] = value
    for w in range(4):
        gout[w] = total(w, d, 0, 0)
    sout[...] = total(4, d, 0, 0)

    def drain(k):
        for w in range(5):
            hop(w, landing(w, k + 1), k + 1, 1).wait_send()

    each(n - 1, drain)
    for c in taround + to_sib:
        c.wait_send()
    to_sib[1].wait_recv()


def reduce_all(n, gain_col, grads, small, table, rows):
    _, _, height, width = grads.shape
    levels = n.bit_length() - 1
    return pl.pallas_call(
        functools.partial(reduce_body, n, gain_col),
        name="reduce_all",
        out_shape=(
            jax.ShapeDtypeStruct((4, height, width), F32),
            jax.ShapeDtypeStruct(small.shape[1:], F32),
            jax.ShapeDtypeStruct(table.shape, F32),
            jax.ShapeDtypeStruct(rows.shape[1:], BF16),
        ),
        in_specs=[vmem_spec()] * 4,
        out_specs=(vmem_spec(),) * 4,
        scratch_shapes=[
            pltpu.VMEM((4, n, height, width), BF16),
            pltpu.VMEM(small.shape, BF16),
            pltpu.VMEM((4, n // 2, height, width) if False else (4, n, height, width), BF16),
            pltpu.VMEM(small.shape, BF16),
            pltpu.VMEM(small.shape, BF16),
            pltpu.VMEM((levels,) + table.shape, F32),
            pltpu.VMEM((levels,) + table.shape, F32),
            pltpu.SemaphoreType.DMA((5, n)),
            pltpu.SemaphoreType.DMA((5, n)),
            pltpu.SemaphoreType.DMA((2 + levels,)),
            pltpu.SemaphoreType.DMA((2 + levels,)),
        ],
        compiler_params=pltpu.CompilerParams(collective_id=3, has_side_effects=True),
    )(grads, small, table, rows)


def dot(left, right, dims, precision=None):
    return lax.dot_general(
        left, right, (dims, ((), ())), precision=precision, preferred_element_type=F32
    )


NN = ((1,), (0,))
NT = ((1,), (1,))
TN = ((0,), (0,))


def gelu_pair(pre):
    c = 0.7978845608028654
    square = pre * pre
    t = jnp.tanh(c * pre * (1.0 + 0.044715 * square))
    half = 0.5 * (1.0 + t)
    value = pre * half
    slope = half + 0.5 * pre * (1.0 - t * t) * c * (1.0 + 3 * 0.044715 * square)
    return value, slope


def local(
    n, tokens, attn_gain, w_query, w_key, w_value, w_proj, rel_table, rel_bucket, segments,
    ffn_gain, router, expert_ids, expert_in, expert_out, cotangent,
):
    half_rows, width = tokens.shape
    seq_len = segments.shape[0]
    experts = router.shape[1]
    capacity = 2 * ((9 * seq_len + 8 * experts - 1) // (8 * experts))
    cap = (capacity + 7) // 8 * 8
    slot_count = experts * cap
    heads = rel_table.shape[1]
    local_width = w_query.shape[1]
    head_dim = local_width // heads
    scale = head_dim ** (-0.5)
    half = width // 2
    m = lax.axis_index("mp")
    lanes = 128

    small = jnp.concatenate(
        [router, ffn_gain[:, None], attn_gain[:, None],
         jnp.zeros((router.shape[0], lanes - experts - 2), BF16)], axis=1)
    full, sfull, stok, scot = gather_all(
        n, w_query, w_key, w_value, w_proj.T, small, tokens, cotangent)
    full = full.reshape(4, width, local_width)
    sfull = sfull.reshape(width, lanes)
    x = stok.reshape(seq_len, width).astype(F32)
    dy = scot.reshape(seq_len, width)
    router_full = sfull[:, :experts]
    gain_two = sfull[:, experts].astype(F32)
    gain_one = sfull[:, experts + 1].astype(F32)

    r_one = lax.rsqrt(jnp.mean(x * x, axis=1, keepdims=True) + EPS)
    xhat_one = x * r_one
    normed_one = (xhat_one * gain_one).astype(BF16)
    q = dot(normed_one, full[0], NN).astype(BF16).reshape(seq_len, heads, head_dim)
    k = dot(normed_one, full[1], NN).astype(BF16).reshape(seq_len, heads, head_dim)
    v = dot(normed_one, full[2], NN).astype(BF16).reshape(seq_len, heads, head_dim)
    pos = jnp.arange(seq_len)
    dist = pos[:, None] - pos[None, :]
    bucket_of = (rel_bucket[:, None] == jnp.arange(rel_table.shape[0])[None, :]).astype(F32)
    by_dist = jnp.dot(bucket_of, rel_table, precision=HIGH)
    bias = jnp.transpose(by_dist[jnp.clip(dist, 0)], (2, 0, 1))
    allowed = (dist >= 0) & (segments[:, None] == segments[None, :])
    logits = jnp.einsum("qhd,khd->hqk", q, k, preferred_element_type=F32) * scale + bias
    logits = jnp.where(allowed[None], logits, NEGATIVE)
    e = jnp.exp(logits - jnp.max(logits, axis=-1, keepdims=True))
    probs = e / jnp.sum(e, axis=-1, keepdims=True)
    probs16 = probs.astype(BF16)
    mixed = jnp.einsum("hqk,khd->qhd", probs16, v, preferred_element_type=F32)
    mixed = mixed.reshape(seq_len, local_width).astype(BF16)
    part = dot(mixed, full[3], NT).astype(BF16)
    after = x + part.astype(F32) + swap(part, 4).astype(F32)

    r_two = lax.rsqrt(jnp.mean(after * after, axis=1, keepdims=True) + EPS)
    xhat_two = after * r_two
    normed_two = (xhat_two * gain_two).astype(BF16)
    r_logits = dot(normed_two, router_full, NN)
    ids = jnp.arange(experts)[None, :]
    member = (expert_ids[:, 0:1] == ids) | (expert_ids[:, 1:2] == ids)
    shifted = jnp.where(member, r_logits, NEGATIVE)
    ex = jnp.exp(shifted - jnp.max(shifted, axis=1, keepdims=True))
    gates = ex / jnp.sum(ex, axis=1, keepdims=True)
    member16 = member.astype(BF16)
    before = dot((dist > 0).astype(BF16), member16, NN)
    before = jnp.where(before < capacity, before, -1.0)
    pick = (
        (before[:, :, None] == jnp.arange(cap, dtype=F32)) & member[:, :, None]
    ).reshape(seq_len, slot_count)
    pick16 = pick.astype(BF16)
    gate_slot = jnp.sum(
        jnp.where(pick.reshape(seq_len, experts, cap), gates[:, :, None], 0.0), axis=0
    ).reshape(slot_count, 1)
    dy16_half = lax.dynamic_slice_in_dim(dy, m * half, half, 1)
    normed_half = lax.dynamic_slice_in_dim(normed_two, m * half, half, 1)
    slots_x = dot(pick16, normed_half, TN).astype(BF16)
    slots_d = (dot(pick16, dy16_half, TN) * gate_slot).astype(BF16)
    slots = jnp.stack([slots_x, slots_d]).reshape(2, experts, cap, half)

    got = dispatch(n, slots)
    in_w, out_w = expert_in[0], expert_out[0]
    rows_x = jnp.concatenate([got[0], got[1]], axis=1)
    rows_d = jnp.concatenate([got[2], got[3]], axis=1)
    pre = dot(rows_x, in_w, NN)
    act, slope = gelu_pair(pre)
    hidden = act.astype(BF16)
    result = dot(hidden, out_w, NN).astype(BF16)
    d_pre = (dot(rows_d, out_w, NT) * slope).astype(BF16)
    grad_out = dot(hidden, rows_d, TN)
    grad_in = dot(rows_x, d_pre, TN)
    d_rows = dot(d_pre, in_w, NT).astype(BF16)
    parts = jnp.stack(
        [result[:, :half], result[:, half:], d_rows[:, :half], d_rows[:, half:]]
    ).reshape(4, n, cap, half)
    ret = collect(n, parts)
    out_slots = jnp.concatenate([ret[0], ret[1]], axis=1)
    dx_slots = jnp.concatenate([ret[2], ret[3]], axis=1)

    weighted = (out_slots.astype(F32) * gate_slot).astype(BF16)
    y = after + dot(pick16, weighted, NN)
    y_mine = lax.dynamic_slice_in_dim(y, m * half_rows, half_rows, 0)
    z = dot(dy, out_slots, NT)
    d_gates = jnp.sum(jnp.where(pick, z, 0.0).reshape(seq_len, experts, cap), axis=2)
    d_router = (gates * (d_gates - jnp.sum(gates * d_gates, axis=1, keepdims=True))).astype(BF16)
    d_normed = dot(pick16, dx_slots, NN) + dot(d_router, router_full, NT)
    g_router = dot(normed_two, d_router, TN)
    g_two = jnp.sum(d_normed * xhat_two, axis=0)
    dn = d_normed * gain_two
    d_after = dy.astype(F32) + r_two * (dn - xhat_two * jnp.mean(dn * xhat_two, axis=1, keepdims=True))
    d_branch = d_after.astype(BF16)
    d_mixed = dot(d_branch, full[3], NN).astype(BF16)
    g_proj = dot(d_branch, mixed, TN)
    d_mixed = d_mixed.reshape(seq_len, heads, head_dim)
    d_probs = jnp.einsum("qhd,khd->hqk", d_mixed, v, preferred_element_type=F32)
    d_logits = (probs * (d_probs - jnp.sum(probs * d_probs, axis=-1, keepdims=True))).astype(BF16)
    dq = (jnp.einsum("hqk,khd->qhd", d_logits, k, preferred_element_type=F32) * scale)
    dk = (jnp.einsum("hqk,qhd->khd", d_logits, q, preferred_element_type=F32) * scale)
    dv = jnp.einsum("hqk,qhd->khd", probs16, d_mixed, preferred_element_type=F32)
    dq, dk, dv = (t.reshape(seq_len, local_width).astype(BF16) for t in (dq, dk, dv))
    onehot = (
        jnp.where(dist >= 0, rel_bucket[jnp.clip(dist, 0)], -1)[None]
        == jnp.arange(rel_table.shape[0])[:, None, None]
    )
    g_table = jnp.einsum("hqk,bqk->hb", d_logits, onehot.astype(BF16), preferred_element_type=F32)
    d_one = dot(dq, full[0], NT) + dot(dk, full[1], NT) + dot(dv, full[2], NT)
    g_one = jnp.sum(d_one * xhat_one, axis=0)
    grads = jnp.stack(
        [dot(normed_one, dq, TN), dot(normed_one, dk, TN), dot(normed_one, dv, TN), g_proj]
    ).astype(BF16).reshape(4, n, width // n, local_width)
    small_grad = jnp.concatenate(
        [g_router, g_two[:, None], g_one[:, None],
         jnp.zeros((width, lanes - experts - 2), F32)], axis=1
    ).astype(BF16).reshape(n, width // n, lanes)
    table = jnp.zeros((8 * ((heads + 7) // 8), lanes), F32).at[:heads, : g_table.shape[1]].set(g_table)

    gsum, ssum, tsum, rsum = reduce_all(
        n, experts + 1, grads, small_grad, table, d_one.astype(BF16).reshape(2, half_rows, width))
    d_one_mine = lax.dynamic_slice_in_dim(d_one, m * half_rows, half_rows, 0) + rsum.astype(F32)
    xh = lax.dynamic_slice_in_dim(xhat_one, m * half_rows, half_rows, 0)
    rr = lax.dynamic_slice_in_dim(r_one, m * half_rows, half_rows, 0)
    da = lax.dynamic_slice_in_dim(d_after, m * half_rows, half_rows, 0)
    dn1 = d_one_mine * gain_one
    grad_tokens = da + rr * (dn1 - xh * jnp.mean(dn1 * xh, axis=1, keepdims=True))
    ssum = lax.dynamic_slice_in_dim(ssum, m * (width // n // 2), width // n // 2, 0)
    return (
        y_mine.astype(BF16),
        grad_tokens,
        ssum[:, experts + 1],
        gsum[0],
        gsum[1],
        gsum[2],
        gsum[3].T,
        tsum[:heads, : rel_table.shape[0]].T,
        ssum[:, experts],
        ssum[:, :experts],
        grad_in[None],
        grad_out[None],
    )


def solution(mesh):
    return jax.shard_map(
        functools.partial(local, mesh.shape["dp"]),
        mesh=mesh,
        in_specs=(
            P(("dp", "mp"), None),
            P(("dp", "mp")),
            P("dp", "mp"),
            P("dp", "mp"),
            P("dp", "mp"),
            P("mp", "dp"),
            P(None, "mp"),
            P(),
            P("dp"),
            P(("dp", "mp")),
            P(("dp", "mp"), None),
            P("dp", None),
            P("dp", None, "mp"),
            P("dp", "mp", None),
            P(("dp", "mp"), None),
        ),
        out_specs=(
            P(("dp", "mp"), None),
            P(("dp", "mp"), None),
            P(("dp", "mp")),
            P("dp", "mp"),
            P("dp", "mp"),
            P("dp", "mp"),
            P("mp", "dp"),
            P(None, "mp"),
            P(("dp", "mp")),
            P(("dp", "mp"), None),
            P("dp", None, "mp"),
            P("dp", "mp", None),
        ),
        check_vma=False,
    )
```
